32 devices in a mesh: shots: 2 (over x), slab: 16 (over z, y, core).
Axes of the slice: x: 2, y: 2, z: 4, core: 2. Of those that a mesh axis runs over, the one named last changes fastest.
Arguments:
- fields: float32 [32, 2, 2, 128, 256], P(('shots', 'slab')), parts along dimension 0, may hold values from -6 to 6
- freq_index: int32 [32], P(('shots', 'slab')), parts along dimension 0, may hold values from 0 to 511
- slowness_index: int32 [16, 128, 256], P('slab'), may hold values from 0 to 255
- slowness_table: float32 [256], replicated, may hold values from 1.2 to 2.4
Outputs:
- image: float32 [32, 128, 256], P(('shots', 'slab')), parts along dimension 0
- fields_out: float32 [32, 2, 2, 128, 256], P(('shots', 'slab')), parts along dimension 0
The draws below stay inside these ranges and needn't reach their ends.
There are 2 independent parts, one for each index of `shots`. The reference program is written for one: setup_inputs(seed, part) draws one part's arguments, and reference() takes and returns one part's arrays. A program takes and returns all parts, laid end to end along the dimension named above; an argument that names none is the same for every part. Nothing has to cross between parts.
All inputs are finite; a program needn't handle non-finite values.
Results may differ from the reference program's by a relative error of at most 0.0003.
Values sent between devices are 32-bit elements; how exact they have to be, the bound alone decides.
A program may use at most 64 MiB of HBM per device.

```python
import jax
import jax.numpy as jnp
from jax import lax

NX = 128
NY = 256
STEPS = 1
TICKS = 3
LEVELS = 256
NFREQ = 512
ITEMS = 16
DEPTH = 16


def touch_ends(values, own_key, low, high):
    spot = [jax.random.randint(jax.random.fold_in(own_key, axis), (), 0, length) for axis, length in enumerate(values.shape)]
    widest = values.shape.index(max(values.shape))
    neighbour = spot[:widest] + [(spot[widest] + 1) % values.shape[widest]] + spot[widest + 1:]
    return values.at[tuple(spot)].set(low).at[tuple(neighbour)].set(high)


def levels(own_key, extent, cuts, least, top_value):
    def one(position, shards_of):
        steps = jax.random.uniform(jax.random.fold_in(jax.random.fold_in(own_key, 6), position), (shards_of,), jnp.float32, least / len(cuts), top_value / len(cuts))
        return jnp.repeat(jnp.exp(steps), extent[position] // shards_of).reshape((-1,) + (1,) * (len(extent) - position - 1))

    factor_of = one(*cuts[0])
    for cut in cuts[1:]:
        factor_of = factor_of * one(*cut)
    return factor_of


def noise(key, shape, deviation, most, split=(), kind=jnp.bfloat16):
    level = levels(key, shape, split, -0.22, 0.18) if split else 1.0
    values = jax.random.normal(key, shape, jnp.float32) * deviation * level
    return jnp.minimum(jnp.maximum(values, -most), most).astype(kind)


def setup_inputs(seed: int = 0, part: int = 0) -> dict:
    key_list = jax.random.split(jax.random.key(seed), 5)
    own_keys = jax.random.split(jax.random.fold_in(key_list[4], part), 5)
    fields = noise(own_keys[0], (ITEMS, 2, 2, NX, NY), 1.0, 6.0, ((0, 16),), jnp.float32)
    freq_index = touch_ends(jax.random.randint(own_keys[1], (ITEMS,), 0, NFREQ), jax.random.fold_in(own_keys[1], 1), 0, NFREQ - 1).astype(jnp.int32)
    slowness_index = touch_ends(jax.random.randint(key_list[2], (DEPTH, NX, NY), 0, LEVELS), jax.random.fold_in(key_list[2], 1), 0, LEVELS - 1).astype(jnp.int32)
    slowness_table = jnp.clip(jax.random.uniform(key_list[3], (LEVELS,), jnp.float32, 1.2, 2.4), 1.2, 2.4)
    return {"fields": fields, "freq_index": freq_index, "slowness_index": slowness_index, "slowness_table": slowness_table}


def advance(real_part, imag_part, omega, plane, mean_slow, signs, wave_sq):
    spectrum = jnp.fft.fft2(lax.complex(real_part, imag_part))
    spec_real = jnp.real(spectrum)
    spec_imag = jnp.imag(spectrum)
    k_square = (omega * mean_slow) ** 2
    vertical = jnp.sqrt(jnp.maximum(k_square - wave_sq, 0.0))
    decay = jnp.sqrt(jnp.maximum(wave_sq - k_square, 0.0))
    damping = jnp.exp(-decay)
    cosine = damping * jnp.cos(vertical)
    sine = signs * damping * jnp.sin(vertical)
    shifted_real = spec_real * cosine - spec_imag * sine
    shifted_imag = spec_real * sine + spec_imag * cosine
    back = jnp.fft.ifft2(lax.complex(shifted_real, shifted_imag))
    back_real = jnp.real(back)
    back_imag = jnp.imag(back)
    screen = omega * (plane - mean_slow)
    screen_cos = jnp.cos(screen)
    screen_sin = signs * jnp.sin(screen)
    return (back_real * screen_cos - back_imag * screen_sin, back_real * screen_sin + back_imag * screen_cos)

def reference(fields, freq_index, slowness_index, slowness_table):
    slow = jnp.take(slowness_table, slowness_index, axis=0)
    mean_slow = lax.optimization_barrier(jnp.mean(slow, axis=(1, 2)))
    planes = slow.reshape(ITEMS, STEPS, NX, NY)
    means = mean_slow.reshape(ITEMS, STEPS)
    omega = 1.0 + freq_index.astype(jnp.float32) / NFREQ
    wave_x = jnp.fft.fftfreq(NX).astype(jnp.float32) * (2.0 * jnp.pi)
    wave_y = jnp.fft.fftfreq(NY).astype(jnp.float32) * (2.0 * jnp.pi)
    wave_sq = wave_x[:, None] ** 2 + wave_y[None, :] ** 2
    signs = jnp.array([1.0, -1.0], dtype=jnp.float32).reshape(2, 1, 1)

    def slab_pass(inputs):
        state, frequency, slab_planes, slab_means = inputs
        real_part = state[:, 0]
        imag_part = state[:, 1]
        images = []
        for depth_no in range(STEPS):
            real_part, imag_part = advance(real_part, imag_part, frequency, slab_planes[depth_no], slab_means[depth_no], signs, wave_sq)
            images.append(real_part[0] * real_part[1] + imag_part[0] * imag_part[1])
        return (jnp.stack([real_part, imag_part], axis=1), jnp.stack(images))
    state = fields
    image_raw = jnp.zeros((DEPTH, NX, NY), dtype=jnp.float32)
    for tick_no in range(TICKS):
        if tick_no > 0:
            state = jnp.concatenate([jnp.zeros_like(state[:1]), state[:-1]], axis=0)
            omega = jnp.concatenate([jnp.zeros_like(omega[:1]), omega[:-1]], axis=0)
        state, added = lax.map(slab_pass, (state, omega, planes, means))
        image_raw = image_raw + added.reshape(DEPTH, NX, NY)
    padded = jnp.pad(image_raw, ((1, 1), (0, 0), (0, 0)))
    image = image_raw - 0.25 * (padded[:-2] + padded[2:])
    return (image, state)
```

```python
import functools
import math

import jax
import jax.numpy as jnp
import numpy as np
from jax import lax
from jax.experimental import pallas as pl
from jax.experimental.pallas import tpu as pltpu
from jax.sharding import PartitionSpec as P

TICKS = 3
NFREQ = 512

F32 = jnp.float32
BF16 = jnp.bfloat16
PI_HI = 3.140625
PI_LO = math.pi - 3.140625


def split_np(mat):
    high = mat.astype(BF16)
    low = (mat - high.astype(np.float64)).astype(BF16)
    return high, low


def dft_tables(nx, ny):
    half = ny // 2
    turn = np.outer(np.arange(nx), np.arange(nx)) % nx * (2.0 * np.pi / nx)
    c, s = np.cos(turn), np.sin(turn)
    x_mats = [np.block([[c, s], [-s, c]]), np.block([[c, -s], [s, c]]) / nx]
    y_mats = []
    for odd in (0, 1):
        turn = np.outer(np.arange(half), 2 * np.arange(half) + odd) % ny * (2.0 * np.pi / ny)
        c, s = np.cos(turn), np.sin(turn)
        y_mats.append(np.block([[c, -s], [s, c]]))
        y_mats.append(np.block([[c.T, s.T], [-s.T, c.T]]) / ny)
    xs = np.stack([part for mat in x_mats for part in split_np(mat)])
    ys = np.stack([part for mat in y_mats for part in split_np(mat)])
    return xs, ys


def split(value):
    high = value.astype(BF16)
    low = (value - high.astype(F32)).astype(BF16)
    return high, low


def dot_data_left(data, high, low):
    d_high, d_low = split(data)
    left = jnp.concatenate([d_high, d_low, d_high], axis=1)
    right = jnp.concatenate([high, high, low], axis=0)
    return jnp.dot(left, right, preferred_element_type=F32)


def dot_data_right(high, low, data):
    d_high, d_low = split(data)
    left = jnp.concatenate([high, high, low], axis=1)
    right = jnp.concatenate([d_high, d_low, d_high], axis=0)
    return jnp.dot(left, right, preferred_element_type=F32)


def sincos(x):
    turns = jnp.floor(x * (1.0 / math.pi) + 0.5)
    r = (x - turns * PI_HI) - turns * PI_LO
    sign = 1.0 - 2.0 * (turns - 2.0 * jnp.floor(turns * 0.5))
    r2 = r * r
    sin_p = 1.0 / math.factorial(11) * -1.0
    for k, sg in ((9, 1.0), (7, -1.0), (5, 1.0), (3, -1.0)):
        sin_p = sin_p * r2 + sg / math.factorial(k)
    sin_p = r + r * (r2 * sin_p)
    cos_p = 1.0 / math.factorial(12)
    for k, sg in ((10, -1.0), (8, 1.0), (6, -1.0), (4, 1.0), (2, -1.0), (0, 1.0)):
        cos_p = cos_p * r2 + sg / math.factorial(k)
    return sign * sin_p, sign * cos_p


def kernel(
    count, fields, freq, sidx, table, xs_in, ys_in, image_out, fields_out,
    held, made, plane, index, levels, xs, ys, raw, low, high, omegas,
    in_sems, send_sems, recv_sems, om_send, om_recv, im_send, im_recv, out_sems,
):
    me = lax.axis_index("slab")
    nx, ny = plane.shape
    half = ny // 2
    has_next = me < count - 1
    has_prev = me > 0
    nxt = jnp.minimum(me + 1, count - 1)
    prv = jnp.maximum(me - 1, 0)

    loads = [
        pltpu.make_async_copy(table, levels, in_sems.at[0]),
        pltpu.make_async_copy(sidx.at[0], index, in_sems.at[1]),
        pltpu.make_async_copy(xs_in, xs, in_sems.at[2]),
        pltpu.make_async_copy(fields.at[0, 0], held.at[0, 0], in_sems.at[3]),
        pltpu.make_async_copy(ys_in, ys, in_sems.at[4]),
        pltpu.make_async_copy(fields.at[0, 1], held.at[0, 1], in_sems.at[5]),
    ]
    for load in loads:
        load.start()

    barrier = pltpu.get_barrier_semaphore()

    @pl.when(has_next)
    def _():
        pl.semaphore_signal(barrier, inc=1, device_id={"slab": nxt})

    @pl.when(has_prev)
    def _():
        pl.semaphore_signal(barrier, inc=1, device_id={"slab": prv})

    def field_copy(tick, f):
        return pltpu.make_async_remote_copy(
            src_ref=made.at[tick, f], dst_ref=held.at[tick + 1, f],
            send_sem=send_sems.at[tick, f], recv_sem=recv_sems.at[tick, f],
            device_id={"slab": nxt},
        )

    def omega_copy(tick):
        return pltpu.make_async_remote_copy(
            src_ref=omegas.at[tick], dst_ref=omegas.at[tick + 1],
            send_sem=om_send.at[tick], recv_sem=om_recv.at[tick],
            device_id={"slab": nxt},
        )

    def image_copy(up):
        return pltpu.make_async_remote_copy(
            src_ref=raw, dst_ref=high if up else low,
            send_sem=im_send.at[up], recv_sem=im_recv.at[up],
            device_id={"slab": prv if up else nxt},
        )

    omegas[0] = jnp.full((8, 128), 1.0 + freq[0].astype(F32) / NFREQ, F32)

    pl.semaphore_wait(barrier, (nxt - me) + (me - prv))

    @pl.when(has_next)
    def _():
        omega_copy(0).start()

    @pl.when(jnp.logical_not(has_prev))
    def _():
        held[1:] = jnp.zeros((TICKS - 1,) + held.shape[1:], F32)
        omegas[1:] = jnp.zeros((TICKS - 1, 8, 128), F32)
        low[...] = jnp.zeros((nx, ny), F32)

    @pl.when(jnp.logical_not(has_next))
    def _():
        high[...] = jnp.zeros((nx, ny), F32)

    loads[0].wait()
    loads[1].wait()
    pieces = [
        jnp.broadcast_to(levels[pl.ds(j * 128, 128)].reshape(1, 128), (nx, 128))
        for j in range(levels.shape[0] // 128)
    ]
    for h in range(ny // 128):
        cols = pl.ds(h * 128, 128)
        idx = index[:, cols]
        inner = idx & 127
        value = jnp.take_along_axis(pieces[0], inner, axis=1, mode="promise_in_bounds")
        for j in range(1, len(pieces)):
            other = jnp.take_along_axis(pieces[j], inner, axis=1, mode="promise_in_bounds")
            value = jnp.where(idx >= j * 128, other, value)
        plane[:, cols] = value
    mean_slow = jnp.sum(plane[...]) * (1.0 / (nx * ny))

    row = lax.broadcasted_iota(jnp.int32, (nx, half), 0)
    wave_x = jnp.where(row < (nx + 1) // 2, row, row - nx).astype(F32) * (2.0 * math.pi / nx)
    lane = lax.broadcasted_iota(jnp.int32, (1, half), 1)

    def phases(omega):
        k_square = (omega * mean_slow) ** 2
        out = []
        for odd in (0, 1):
            k = 2 * lane + odd
            wave_y = jnp.where(k < (ny + 1) // 2, k, k - ny).astype(F32) * (2.0 * math.pi / ny)
            q = k_square - (wave_x * wave_x + wave_y * wave_y)
            root = jnp.sqrt(jnp.abs(q))
            sin_v, cos_v = sincos(root)
            moving = q > 0.0
            out.append((
                jnp.where(moving, cos_v, jnp.exp(-root)),
                jnp.where(moving, sin_v, 0.0),
            ))
        return out

    def step(tick, f, phase, screen):
        re, im = held[tick, f, 0], held[tick, f, 1]
        sg = 1.0 if f == 0 else -1.0
        spec = dot_data_right(xs[0], xs[1], jnp.concatenate([re, im], axis=0))
        left, right = spec[:, :half], spec[:, half:]
        back = []
        for odd, mix in ((0, left + right), (1, left - right)):
            cos_p, sin_p = phase[odd]
            sin_p = sg * sin_p
            fwd = dot_data_left(
                jnp.concatenate([mix[:nx], mix[nx:]], axis=1), ys[4 * odd], ys[4 * odd + 1]
            )
            v_re, v_im = fwd[:, :half], fwd[:, half:]
            moved = jnp.concatenate(
                [v_re * cos_p - v_im * sin_p, v_re * sin_p + v_im * cos_p], axis=1
            )
            back.append(dot_data_left(moved, ys[4 * odd + 2], ys[4 * odd + 3]))
        plus, minus = back[0] + back[1], back[0] - back[1]
        cols = jnp.concatenate([
            jnp.concatenate([plus[:, :half], minus[:, :half]], axis=1),
            jnp.concatenate([plus[:, half:], minus[:, half:]], axis=1),
        ], axis=0)
        field = dot_data_right(xs[2], xs[3], cols)
        b_re, b_im = field[:nx], field[nx:]
        s_sin, s_cos = screen
        s_sin = sg * s_sin
        made[tick, f, 0] = b_re * s_cos - b_im * s_sin
        made[tick, f, 1] = b_re * s_sin + b_im * s_cos

    def write_out(f):
        return pltpu.make_async_copy(made.at[TICKS - 1, f], fields_out.at[0, f], out_sems.at[f])

    for tick in range(TICKS):
        if tick > 0:
            @pl.when(has_prev)
            def _():
                omega_copy(tick - 1).wait_recv()

            if tick < TICKS - 1:
                @pl.when(has_next)
                def _():
                    omega_copy(tick).start()
        omega = omegas[tick][:1]
        phase = phases(omega)
        omega_wide = jnp.concatenate([omega] * (ny // 128), axis=1)
        screen = sincos(omega_wide * (plane[...] - mean_slow))
        if tick == 0:
            loads[2].wait()
        for f in (0, 1):
            if tick == 0:
                loads[3 + 2 * f].wait()
                if f == 0:
                    loads[4].wait()
            else:
                @pl.when(has_prev)
                def _():
                    field_copy(tick - 1, f).wait_recv()
            step(tick, f, phase, screen)
            if tick < TICKS - 1:
                @pl.when(has_next)
                def _():
                    field_copy(tick, f).start()
            else:
                write_out(f).start()
        added = made[tick, 0, 0] * made[tick, 1, 0] + made[tick, 0, 1] * made[tick, 1, 1]
        raw[...] = added if tick == 0 else raw[...] + added

    @pl.when(has_next)
    def _():
        image_copy(0).start()

    @pl.when(has_prev)
    def _():
        image_copy(1).start()

    @pl.when(has_prev)
    def _():
        image_copy(0).wait_recv()

    @pl.when(has_next)
    def _():
        image_copy(1).wait_recv()

    plane[...] = raw[...] - 0.25 * (low[...] + high[...])
    last = pltpu.make_async_copy(plane, image_out.at[0], out_sems.at[2])
    last.start()

    @pl.when(has_next)
    def _():
        for tick in range(TICKS - 1):
            omega_copy(tick).wait_send()
            for f in (0, 1):
                field_copy(tick, f).wait_send()
        image_copy(0).wait_send()

    @pl.when(has_prev)
    def _():
        image_copy(1).wait_send()

    write_out(0).wait()
    write_out(1).wait()
    last.wait()


def body(fields, freq_index, slowness_index, slowness_table):
    nx, ny = slowness_index.shape[1:]
    assert slowness_index.shape[0] == 1
    xs, ys = dft_tables(nx, ny)
    count = lax.axis_size("slab")
    any_spec = pl.BlockSpec(memory_space=pl.ANY)
    return pl.pallas_call(
        functools.partial(kernel, count),
        out_shape=(
            jax.ShapeDtypeStruct((1, nx, ny), F32),
            jax.ShapeDtypeStruct(fields.shape, F32),
        ),
        in_specs=[
            any_spec, pl.BlockSpec(memory_space=pltpu.SMEM), any_spec, any_spec, any_spec, any_spec,
        ],
        out_specs=(any_spec, any_spec),
        scratch_shapes=[
            pltpu.VMEM((TICKS, 2, 2, nx, ny), F32),
            pltpu.VMEM((TICKS, 2, 2, nx, ny), F32),
            pltpu.VMEM((nx, ny), F32),
            pltpu.VMEM((nx, ny), jnp.int32),
            pltpu.VMEM(slowness_table.shape, F32),
            pltpu.VMEM(xs.shape, BF16),
            pltpu.VMEM(ys.shape, BF16),
            pltpu.VMEM((nx, ny), F32),
            pltpu.VMEM((nx, ny), F32),
            pltpu.VMEM((nx, ny), F32),
            pltpu.VMEM((TICKS, 8, 128), F32),
            pltpu.SemaphoreType.DMA((6,)),
            pltpu.SemaphoreType.DMA((TICKS - 1, 2)),
            pltpu.SemaphoreType.DMA((TICKS - 1, 2)),
            pltpu.SemaphoreType.DMA((TICKS - 1,)),
            pltpu.SemaphoreType.DMA((TICKS - 1,)),
            pltpu.SemaphoreType.DMA((2,)),
            pltpu.SemaphoreType.DMA((2,)),
            pltpu.SemaphoreType.DMA((3,)),
        ],
        compiler_params=pltpu.CompilerParams(collective_id=0, has_side_effects=True),
        name="slabs",
    )(fields, freq_index, slowness_index, slowness_table, jnp.asarray(xs), jnp.asarray(ys))


def solution(mesh):
    return jax.shard_map(
        body,
        mesh=mesh,
        in_specs=(
            P(("shots", "slab"), None, None, None, None),
            P(("shots", "slab")),
            P("slab", None, None),
            P(),
        ),
        out_specs=(P(("shots", "slab"), None, None), P(("shots", "slab"), None, None, None, None)),
        check_vma=False,
    )
```

```python
import functools
import math

import jax
import jax.numpy as jnp
import numpy as np
from jax import lax
from jax.experimental import pallas as pl
from jax.experimental.pallas import tpu as pltpu
from jax.sharding import PartitionSpec as P

TICKS = 3
NFREQ = 512

F32 = jnp.float32
BF16 = jnp.bfloat16
PI_HI = 3.140625
PI_LO = math.pi - 3.140625


def split_np(mat):
    high = mat.astype(BF16)
    low = (mat - high.astype(np.float64)).astype(BF16)
    return high, low


def dft_tables(nx, ny):
    half = ny // 2
    turn = np.outer(np.arange(nx), np.arange(nx)) % nx * (2.0 * np.pi / nx)
    c, s = np.cos(turn), np.sin(turn)
    x_mats = [np.block([[c, s], [-s, c]]), np.block([[c, -s], [s, c]]) / nx]
    y_mats = []
    for odd in (0, 1):
        turn = np.outer(np.arange(half), 2 * np.arange(half) + odd) % ny * (2.0 * np.pi / ny)
        c, s = np.cos(turn), np.sin(turn)
        y_mats.append(np.block([[c, -s], [s, c]]))
        y_mats.append(np.block([[c.T, s.T], [-s.T, c.T]]) / ny)
    xs = np.stack([part for mat in x_mats for part in split_np(mat)])
    ys = np.stack([part for mat in y_mats for part in split_np(mat)])
    return xs, ys


def split(value):
    high = value.astype(BF16)
    low = (value - high.astype(F32)).astype(BF16)
    return high, low


def dot_data_left(data, high, low):
    d_high, d_low = split(data)
    left = jnp.concatenate([d_high, d_low, d_high], axis=1)
    right = jnp.concatenate([high, high, low], axis=0)
    return jnp.dot(left, right, preferred_element_type=F32)


def dot_data_right(high, low, data):
    d_high, d_low = split(data)
    left = jnp.concatenate([high, high, low], axis=1)
    right = jnp.concatenate([d_high, d_low, d_high], axis=0)
    return jnp.dot(left, right, preferred_element_type=F32)


def sincos(x):
    turns = jnp.floor(x * (1.0 / math.pi) + 0.5)
    r = (x - turns * PI_HI) - turns * PI_LO
    sign = 1.0 - 2.0 * (turns - 2.0 * jnp.floor(turns * 0.5))
    r2 = r * r
    sin_p = 1.0 / math.factorial(11) * -1.0
    for k, sg in ((9, 1.0), (7, -1.0), (5, 1.0), (3, -1.0)):
        sin_p = sin_p * r2 + sg / math.factorial(k)
    sin_p = r + r * (r2 * sin_p)
    cos_p = 1.0 / math.factorial(12)
    for k, sg in ((10, -1.0), (8, 1.0), (6, -1.0), (4, 1.0), (2, -1.0), (0, 1.0)):
        cos_p = cos_p * r2 + sg / math.factorial(k)
    return sign * sin_p, sign * cos_p


def kernel(
    count, fields, freq, sidx, table, xs_in, ys_in, image_out, fields_out,
    held, made, plane, index, levels, xs, ys, raw, low, high, omegas,
    in_sems, send_sems, recv_sems, om_send, om_recv, im_send, im_recv,
):
    me = lax.axis_index("slab")
    nx, ny = plane.shape
    half = ny // 2
    has_next = me < count - 1
    has_prev = me > 0
    nxt = jnp.minimum(me + 1, count - 1)
    prv = jnp.maximum(me - 1, 0)

    loads = [
        pltpu.make_async_copy(table, levels, in_sems.at[0]),
        pltpu.make_async_copy(sidx.at[0], index, in_sems.at[1]),
        pltpu.make_async_copy(xs_in, xs, in_sems.at[2]),
        pltpu.make_async_copy(fields.at[0, 0], held.at[0, 0], in_sems.at[3]),
        pltpu.make_async_copy(ys_in, ys, in_sems.at[4]),
        pltpu.make_async_copy(fields.at[0, 1], held.at[0, 1], in_sems.at[5]),
    ]
    for load in loads:
        load.start()

    barrier = pltpu.get_barrier_semaphore()

    @pl.when(has_next)
    def _():
        pl.semaphore_signal(barrier, inc=1, device_id={"slab": nxt})

    @pl.when(has_prev)
    def _():
        pl.semaphore_signal(barrier, inc=1, device_id={"slab": prv})

    def field_copy(tick, f):
        return pltpu.make_async_remote_copy(
            src_ref=made.at[tick, f], dst_ref=held.at[tick + 1, f],
            send_sem=send_sems.at[tick, f], recv_sem=recv_sems.at[tick, f],
            device_id={"slab": nxt},
        )

    def omega_copy(tick):
        return pltpu.make_async_remote_copy(
            src_ref=omegas.at[tick], dst_ref=omegas.at[tick + 1],
            send_sem=om_send.at[tick], recv_sem=om_recv.at[tick],
            device_id={"slab": nxt},
        )

    def image_copy(up):
        return pltpu.make_async_remote_copy(
            src_ref=raw, dst_ref=high if up else low,
            send_sem=im_send.at[up], recv_sem=im_recv.at[up],
            device_id={"slab": prv if up else nxt},
        )

    omegas[0] = jnp.full((8, 128), 1.0 + freq[0].astype(F32) / NFREQ, F32)

    pl.semaphore_wait(barrier, (nxt - me) + (me - prv))

    @pl.when(has_next)
    def _():
        omega_copy(0).start()

    @pl.when(jnp.logical_not(has_prev))
    def _():
        held[1:] = jnp.zeros((TICKS - 1,) + held.shape[1:], F32)
        omegas[1:] = jnp.zeros((TICKS - 1, 8, 128), F32)
        low[...] = jnp.zeros((nx, ny), F32)

    @pl.when(jnp.logical_not(has_next))
    def _():
        high[...] = jnp.zeros((nx, ny), F32)

    loads[0].wait()
    loads[1].wait()
    pieces = [
        jnp.broadcast_to(levels[pl.ds(j * 128, 128)].reshape(1, 128), (nx, 128))
        for j in range(levels.shape[0] // 128)
    ]
    for h in range(ny // 128):
        cols = pl.ds(h * 128, 128)
        idx = index[:, cols]
        inner = idx & 127
        value = jnp.take_along_axis(pieces[0], inner, axis=1, mode="promise_in_bounds")
        for j in range(1, len(pieces)):
            other = jnp.take_along_axis(pieces[j], inner, axis=1, mode="promise_in_bounds")
            value = jnp.where(idx >= j * 128, other, value)
        plane[:, cols] = value
    mean_slow = jnp.sum(plane[...]) * (1.0 / (nx * ny))

    row = lax.broadcasted_iota(jnp.int32, (nx, half), 0)
    wave_x = jnp.where(row < (nx + 1) // 2, row, row - nx).astype(F32) * (2.0 * math.pi / nx)
    lane = lax.broadcasted_iota(jnp.int32, (1, half), 1)

    def phases(omega):
        k_square = (omega * mean_slow) ** 2
        out = []
        for odd in (0, 1):
            k = 2 * lane + odd
            wave_y = jnp.where(k < (ny + 1) // 2, k, k - ny).astype(F32) * (2.0 * math.pi / ny)
            q = k_square - (wave_x * wave_x + wave_y * wave_y)
            root = jnp.sqrt(jnp.abs(q))
            sin_v, cos_v = sincos(root)
            moving = q > 0.0
            out.append((
                jnp.where(moving, cos_v, jnp.exp(-root)),
                jnp.where(moving, sin_v, 0.0),
            ))
        return out

    def step(tick, f, phase, screen):
        re, im = held[tick, f, 0], held[tick, f, 1]
        sg = 1.0 if f == 0 else -1.0
        spec = dot_data_right(xs[0], xs[1], jnp.concatenate([re, im], axis=0))
        left, right = spec[:, :half], spec[:, half:]
        back = []
        for odd, mix in ((0, left + right), (1, left - right)):
            cos_p, sin_p = phase[odd]
            sin_p = sg * sin_p
            fwd = dot_data_left(
                jnp.concatenate([mix[:nx], mix[nx:]], axis=1), ys[4 * odd], ys[4 * odd + 1]
            )
            v_re, v_im = fwd[:, :half], fwd[:, half:]
            moved = jnp.concatenate(
                [v_re * cos_p - v_im * sin_p, v_re * sin_p + v_im * cos_p], axis=1
            )
            back.append(dot_data_left(moved, ys[4 * odd + 2], ys[4 * odd + 3]))
        plus, minus = back[0] + back[1], back[0] - back[1]
        cols = jnp.concatenate([
            jnp.concatenate([plus[:, :half], minus[:, :half]], axis=1),
            jnp.concatenate([plus[:, half:], minus[:, half:]], axis=1),
        ], axis=0)
        field = dot_data_right(xs[2], xs[3], cols)
        b_re, b_im = field[:nx], field[nx:]
        s_sin, s_cos = screen
        s_sin = sg * s_sin
        target = moved_fields(tick)
        target[f, 0] = b_re * s_cos - b_im * s_sin
        target[f, 1] = b_re * s_sin + b_im * s_cos

    def moved_fields(tick):
        return made.at[tick] if tick < TICKS - 1 else fields_out.at[0]

    for tick in range(TICKS):
        if tick > 0:
            @pl.when(has_prev)
            def _():
                omega_copy(tick - 1).wait_recv()

            if tick < TICKS - 1:
                @pl.when(has_next)
                def _():
                    omega_copy(tick).start()
        omega = omegas[tick][:1]
        phase = phases(omega)
        omega_wide = jnp.concatenate([omega] * (ny // 128), axis=1)
        screen = sincos(omega_wide * (plane[...] - mean_slow))
        if tick == 0:
            loads[2].wait()
        for f in (0, 1):
            if tick == 0:
                loads[3 + 2 * f].wait()
                if f == 0:
                    loads[4].wait()
            else:
                @pl.when(has_prev)
                def _():
                    field_copy(tick - 1, f).wait_recv()
            step(tick, f, phase, screen)
            if tick < TICKS - 1:
                @pl.when(has_next)
                def _():
                    field_copy(tick, f).start()
        now = moved_fields(tick)
        added = now[0, 0] * now[1, 0] + now[0, 1] * now[1, 1]
        raw[...] = added if tick == 0 else raw[...] + added

    @pl.when(has_next)
    def _():
        image_copy(0).start()

    @pl.when(has_prev)
    def _():
        image_copy(1).start()

    @pl.when(has_prev)
    def _():
        image_copy(0).wait_recv()

    @pl.when(has_next)
    def _():
        image_copy(1).wait_recv()

    image_out[0] = raw[...] - 0.25 * (low[...] + high[...])

    @pl.when(has_next)
    def _():
        for tick in range(TICKS - 1):
            omega_copy(tick).wait_send()
            for f in (0, 1):
                field_copy(tick, f).wait_send()
        image_copy(0).wait_send()

    @pl.when(has_prev)
    def _():
        image_copy(1).wait_send()


def store(image, fields, image_out, fields_out, sems):
    copies = [
        pltpu.make_async_copy(fields, fields_out, sems.at[0]),
        pltpu.make_async_copy(image, image_out, sems.at[1]),
    ]
    for copy in copies:
        copy.start()
    for copy in copies:
        copy.wait()


def body(fields, freq_index, slowness_index, slowness_table):
    nx, ny = slowness_index.shape[1:]
    assert slowness_index.shape[0] == 1
    xs, ys = dft_tables(nx, ny)
    count = lax.axis_size("slab")
    any_spec = pl.BlockSpec(memory_space=pl.ANY)
    vmem_spec = pl.BlockSpec(memory_space=pltpu.VMEM)
    image, moved = pl.pallas_call(
        functools.partial(kernel, count),
        out_shape=(pltpu.VMEM((1, nx, ny), F32), pltpu.VMEM(fields.shape, F32)),
        in_specs=[
            any_spec, pl.BlockSpec(memory_space=pltpu.SMEM), any_spec, any_spec, any_spec, any_spec,
        ],
        out_specs=(vmem_spec, vmem_spec),
        scratch_shapes=[
            pltpu.VMEM((TICKS, 2, 2, nx, ny), F32),
            pltpu.VMEM((TICKS - 1, 2, 2, nx, ny), F32),
            pltpu.VMEM((nx, ny), F32),
            pltpu.VMEM((nx, ny), jnp.int32),
            pltpu.VMEM(slowness_table.shape, F32),
            pltpu.VMEM(xs.shape, BF16),
            pltpu.VMEM(ys.shape, BF16),
            pltpu.VMEM((nx, ny), F32),
            pltpu.VMEM((nx, ny), F32),
            pltpu.VMEM((nx, ny), F32),
            pltpu.VMEM((TICKS, 8, 128), F32),
            pltpu.SemaphoreType.DMA((6,)),
            pltpu.SemaphoreType.DMA((TICKS - 1, 2)),
            pltpu.SemaphoreType.DMA((TICKS - 1, 2)),
            pltpu.SemaphoreType.DMA((TICKS - 1,)),
            pltpu.SemaphoreType.DMA((TICKS - 1,)),
            pltpu.SemaphoreType.DMA((2,)),
            pltpu.SemaphoreType.DMA((2,)),
        ],
        compiler_params=pltpu.CompilerParams(collective_id=0, has_side_effects=True),
        name="slabs",
    )(fields, freq_index, slowness_index, slowness_table, jnp.asarray(xs), jnp.asarray(ys))
    return pl.pallas_call(
        store,
        out_shape=(
            jax.ShapeDtypeStruct((1, nx, ny), F32),
            jax.ShapeDtypeStruct(fields.shape, F32),
        ),
        in_specs=[vmem_spec, vmem_spec],
        out_specs=(any_spec, any_spec),
        scratch_shapes=[pltpu.SemaphoreType.DMA((2,))],
        name="store",
    )(
        pltpu.with_memory_space_constraint(image, pltpu.VMEM),
        pltpu.with_memory_space_constraint(moved, pltpu.VMEM),
    )


def solution(mesh):
    return jax.shard_map(
        body,
        mesh=mesh,
        in_specs=(
            P(("shots", "slab"), None, None, None, None),
            P(("shots", "slab")),
            P("slab", None, None),
            P(),
        ),
        out_specs=(P(("shots", "slab"), None, None), P(("shots", "slab"), None, None, None, None)),
        check_vma=False,
    )
```

```python
import functools
import math

import jax
import jax.numpy as jnp
import numpy as np
from jax import lax
from jax.experimental import pallas as pl
from jax.experimental.pallas import tpu as pltpu
from jax.sharding import PartitionSpec as P

TICKS = 3
NFREQ = 512

F32 = jnp.float32
BF16 = jnp.bfloat16
PI_HI = 3.140625
PI_LO = math.pi - 3.140625


def split_np(mat):
    high = mat.astype(BF16)
    low = (mat - high.astype(np.float64)).astype(BF16)
    return high, low


def dft_tables(nx, ny):
    half = ny // 2
    turn = np.outer(np.arange(nx), np.arange(nx)) % nx * (2.0 * np.pi / nx)
    c, s = np.cos(turn), np.sin(turn)
    x_mats = [np.block([[c, s], [-s, c]]), np.block([[c, -s], [s, c]]) / nx]
    y_mats = []
    for odd in (0, 1):
        turn = np.outer(np.arange(half), 2 * np.arange(half) + odd) % ny * (2.0 * np.pi / ny)
        c, s = np.cos(turn), np.sin(turn)
        y_mats.append(np.block([[c, -s], [s, c]]))
        y_mats.append(np.block([[c.T, s.T], [-s.T, c.T]]) / ny)
    xs = np.stack([part for mat in x_mats for part in split_np(mat)])
    ys = np.stack([part for mat in y_mats for part in split_np(mat)])
    return xs, ys


def split(value):
    high = value.astype(BF16)
    low = (value - high.astype(F32)).astype(BF16)
    return high, low


def dot_data_left(data, high, low):
    d_high, d_low = split(data)
    left = jnp.concatenate([d_high, d_low, d_high], axis=1)
    right = jnp.concatenate([high, high, low], axis=0)
    return jnp.dot(left, right, preferred_element_type=F32)


def dot_data_right(high, low, data):
    d_high, d_low = split(data)
    left = jnp.concatenate([high, high, low], axis=1)
    right = jnp.concatenate([d_high, d_low, d_high], axis=0)
    return jnp.dot(left, right, preferred_element_type=F32)


def sincos(x):
    turns = jnp.floor(x * (1.0 / math.pi) + 0.5)
    r = (x - turns * PI_HI) - turns * PI_LO
    sign = 1.0 - 2.0 * (turns - 2.0 * jnp.floor(turns * 0.5))
    r2 = r * r
    sin_p = 1.0 / math.factorial(11) * -1.0
    for k, sg in ((9, 1.0), (7, -1.0), (5, 1.0), (3, -1.0)):
        sin_p = sin_p * r2 + sg / math.factorial(k)
    sin_p = r + r * (r2 * sin_p)
    cos_p = 1.0 / math.factorial(12)
    for k, sg in ((10, -1.0), (8, 1.0), (6, -1.0), (4, 1.0), (2, -1.0), (0, 1.0)):
        cos_p = cos_p * r2 + sg / math.factorial(k)
    return sign * sin_p, sign * cos_p


def kernel(
    count, fields, freq, sidx, table, xs_in, ys_in, image_out, fields_out,
    held, made, plane, index, levels, xs, ys, raw, low, high, omegas,
    index_next, plane_next, ahead, bonus, part,
    in_sems, send_sems, recv_sems, om_send, om_recv, im_send, im_recv, ix_send, ix_recv,
):
    me = lax.axis_index("slab")
    nx, ny = plane.shape
    half = ny // 2
    has_next = me < count - 1
    has_prev = me > 0
    nxt = jnp.minimum(me + 1, count - 1)
    prv = jnp.maximum(me - 1, 0)
    odd = lax.rem(me, 2) == 1
    looks_ahead = jnp.logical_and(odd, has_next)
    is_looked = jnp.logical_and(jnp.logical_not(odd), has_prev)

    loads = [
        pltpu.make_async_copy(table, levels, in_sems.at[0]),
        pltpu.make_async_copy(sidx.at[0], index, in_sems.at[1]),
        pltpu.make_async_copy(xs_in, xs, in_sems.at[2]),
        pltpu.make_async_copy(fields.at[0, 0], held.at[0, 0], in_sems.at[3]),
        pltpu.make_async_copy(ys_in, ys, in_sems.at[4]),
        pltpu.make_async_copy(fields.at[0, 1], held.at[0, 1], in_sems.at[5]),
    ]
    for load in loads:
        load.start()

    barrier = pltpu.get_barrier_semaphore()

    @pl.when(has_next)
    def _():
        pl.semaphore_signal(barrier, inc=1, device_id={"slab": nxt})

    @pl.when(has_prev)
    def _():
        pl.semaphore_signal(barrier, inc=1, device_id={"slab": prv})

    def field_copy(tick, f):
        return pltpu.make_async_remote_copy(
            src_ref=made.at[tick, f], dst_ref=held.at[tick + 1, f],
            send_sem=send_sems.at[tick, f], recv_sem=recv_sems.at[tick, f],
            device_id={"slab": nxt},
        )

    def omega_copy(tick):
        return pltpu.make_async_remote_copy(
            src_ref=omegas.at[tick], dst_ref=omegas.at[tick + 1],
            send_sem=om_send.at[tick], recv_sem=om_recv.at[tick],
            device_id={"slab": nxt},
        )

    def index_copy():
        return pltpu.make_async_remote_copy(
            src_ref=sidx.at[0], dst_ref=index_next,
            send_sem=ix_send, recv_sem=ix_recv, device_id={"slab": prv},
        )

    def image_copy(up, source=raw):
        return pltpu.make_async_remote_copy(
            src_ref=source, dst_ref=high if up else low,
            send_sem=im_send.at[up], recv_sem=im_recv.at[up],
            device_id={"slab": prv if up else nxt},
        )

    omegas[0] = jnp.full((8, 128), 1.0 + freq[0].astype(F32) / NFREQ, F32)

    pl.semaphore_wait(barrier, (nxt - me) + (me - prv))

    @pl.when(is_looked)
    def _():
        index_copy().start()

    @pl.when(has_next)
    def _():
        omega_copy(0).start()

    @pl.when(jnp.logical_not(has_prev))
    def _():
        held[1:] = jnp.zeros((TICKS - 1,) + held.shape[1:], F32)
        omegas[1:] = jnp.zeros((TICKS - 1, 8, 128), F32)
        low[...] = jnp.zeros((nx, ny), F32)

    @pl.when(jnp.logical_not(has_next))
    def _():
        high[...] = jnp.zeros((nx, ny), F32)

    loads[0].wait()
    loads[1].wait()
    pieces = [
        jnp.broadcast_to(levels[pl.ds(j * 128, 128)].reshape(1, 128), (nx, 128))
        for j in range(levels.shape[0] // 128)
    ]

    def lookup(index, plane):
        for h in range(ny // 128):
            cols = pl.ds(h * 128, 128)
            idx = index[:, cols]
            inner = idx & 127
            value = jnp.take_along_axis(pieces[0], inner, axis=1, mode="promise_in_bounds")
            for j in range(1, len(pieces)):
                other = jnp.take_along_axis(pieces[j], inner, axis=1, mode="promise_in_bounds")
                value = jnp.where(idx >= j * 128, other, value)
            plane[:, cols] = value
        return jnp.sum(plane[...]) * (1.0 / (nx * ny))

    mean_slow = lookup(index, plane)

    row = lax.broadcasted_iota(jnp.int32, (nx, half), 0)
    wave_x = jnp.where(row < (nx + 1) // 2, row, row - nx).astype(F32) * (2.0 * math.pi / nx)
    lane = lax.broadcasted_iota(jnp.int32, (1, half), 1)

    def phases(omega, mean_slow):
        k_square = (omega * mean_slow) ** 2
        out = []
        for odd in (0, 1):
            k = 2 * lane + odd
            wave_y = jnp.where(k < (ny + 1) // 2, k, k - ny).astype(F32) * (2.0 * math.pi / ny)
            q = k_square - (wave_x * wave_x + wave_y * wave_y)
            root = jnp.sqrt(jnp.abs(q))
            sin_v, cos_v = sincos(root)
            moving = q > 0.0
            out.append((
                jnp.where(moving, cos_v, jnp.exp(-root)),
                jnp.where(moving, sin_v, 0.0),
            ))
        return out

    def step(source, target, f, phase, screen):
        re, im = source[f, 0], source[f, 1]
        sg = 1.0 if f == 0 else -1.0
        spec = dot_data_right(xs[0], xs[1], jnp.concatenate([re, im], axis=0))
        left, right = spec[:, :half], spec[:, half:]
        back = []
        for odd, mix in ((0, left + right), (1, left - right)):
            cos_p, sin_p = phase[odd]
            sin_p = sg * sin_p
            fwd = dot_data_left(
                jnp.concatenate([mix[:nx], mix[nx:]], axis=1), ys[4 * odd], ys[4 * odd + 1]
            )
            v_re, v_im = fwd[:, :half], fwd[:, half:]
            moved = jnp.concatenate(
                [v_re * cos_p - v_im * sin_p, v_re * sin_p + v_im * cos_p], axis=1
            )
            back.append(dot_data_left(moved, ys[4 * odd + 2], ys[4 * odd + 3]))
        plus, minus = back[0] + back[1], back[0] - back[1]
        cols = jnp.concatenate([
            jnp.concatenate([plus[:, :half], minus[:, :half]], axis=1),
            jnp.concatenate([plus[:, half:], minus[:, half:]], axis=1),
        ], axis=0)
        field = dot_data_right(xs[2], xs[3], cols)
        b_re, b_im = field[:nx], field[nx:]
        s_sin, s_cos = screen
        s_sin = sg * s_sin
        target[f, 0] = b_re * s_cos - b_im * s_sin
        target[f, 1] = b_re * s_sin + b_im * s_cos

    def moved_fields(tick):
        return made.at[tick] if tick < TICKS - 1 else fields_out.at[0]

    def factors(omega, plane, mean_slow):
        omega_wide = jnp.concatenate([omega] * (ny // 128), axis=1)
        return phases(omega, mean_slow), sincos(omega_wide * (plane[...] - mean_slow))

    for tick in range(TICKS):
        if tick > 0:
            @pl.when(has_prev)
            def _():
                omega_copy(tick - 1).wait_recv()

            if tick < TICKS - 1:
                @pl.when(has_next)
                def _():
                    omega_copy(tick).start()
        phase, screen = factors(omegas[tick][:1], plane, mean_slow)
        if tick == 0:
            loads[2].wait()
        for f in (0, 1):
            if tick == 0:
                loads[3 + 2 * f].wait()
                if f == 0:
                    loads[4].wait()
            else:
                @pl.when(has_prev)
                def _():
                    field_copy(tick - 1, f).wait_recv()
            if tick == TICKS - 1 and f == 0:
                @pl.when(is_looked)
                def _():
                    image_copy(1, part).start()
            step(held.at[tick], moved_fields(tick), f, phase, screen)
            if tick < TICKS - 1:
                @pl.when(has_next)
                def _():
                    field_copy(tick, f).start()
        now = moved_fields(tick)
        added = now[0, 0] * now[1, 0] + now[0, 1] * now[1, 1]
        raw[...] = added if tick == 0 else raw[...] + added
        if tick == TICKS - 2:
            part[...] = raw[...]

            @pl.when(looks_ahead)
            def _():
                index_copy().wait_recv()
                mean_next = lookup(index_next, plane_next)
                phase, screen = factors(omegas[tick][:1], plane_next, mean_next)
                for f in (0, 1):
                    step(made.at[tick], ahead, f, phase, screen)
                bonus[...] = ahead[0, 0] * ahead[1, 0] + ahead[0, 1] * ahead[1, 1]

            @pl.when(jnp.logical_not(looks_ahead))
            def _():
                bonus[...] = jnp.zeros((nx, ny), F32)

    @pl.when(has_next)
    def _():
        image_copy(0).start()

    @pl.when(odd)
    def _():
        image_copy(1).start()

    @pl.when(has_prev)
    def _():
        image_copy(0).wait_recv()

    @pl.when(has_next)
    def _():
        image_copy(1).wait_recv()

    image_out[0] = raw[...] - 0.25 * (low[...] + (high[...] + bonus[...]))

    @pl.when(has_next)
    def _():
        for tick in range(TICKS - 1):
            omega_copy(tick).wait_send()
            for f in (0, 1):
                field_copy(tick, f).wait_send()
        image_copy(0).wait_send()

    @pl.when(odd)
    def _():
        image_copy(1).wait_send()

    @pl.when(is_looked)
    def _():
        index_copy().wait_send()
        image_copy(1, part).wait_send()


def store(image, fields, image_out, fields_out, sems):
    copies = [
        pltpu.make_async_copy(fields, fields_out, sems.at[0]),
        pltpu.make_async_copy(image, image_out, sems.at[1]),
    ]
    for copy in copies:
        copy.start()
    for copy in copies:
        copy.wait()


def body(fields, freq_index, slowness_index, slowness_table):
    nx, ny = slowness_index.shape[1:]
    assert slowness_index.shape[0] == 1
    xs, ys = dft_tables(nx, ny)
    count = lax.axis_size("slab")
    any_spec = pl.BlockSpec(memory_space=pl.ANY)
    vmem_spec = pl.BlockSpec(memory_space=pltpu.VMEM)
    image, moved = pl.pallas_call(
        functools.partial(kernel, count),
        out_shape=(pltpu.VMEM((1, nx, ny), F32), pltpu.VMEM(fields.shape, F32)),
        in_specs=[
            any_spec, pl.BlockSpec(memory_space=pltpu.SMEM), any_spec, any_spec, any_spec, any_spec,
        ],
        out_specs=(vmem_spec, vmem_spec),
        scratch_shapes=[
            pltpu.VMEM((TICKS, 2, 2, nx, ny), F32),
            pltpu.VMEM((TICKS - 1, 2, 2, nx, ny), F32),
            pltpu.VMEM((nx, ny), F32),
            pltpu.VMEM((nx, ny), jnp.int32),
            pltpu.VMEM(slowness_table.shape, F32),
            pltpu.VMEM(xs.shape, BF16),
            pltpu.VMEM(ys.shape, BF16),
            pltpu.VMEM((nx, ny), F32),
            pltpu.VMEM((nx, ny), F32),
            pltpu.VMEM((nx, ny), F32),
            pltpu.VMEM((TICKS, 8, 128), F32),
            pltpu.VMEM((nx, ny), jnp.int32),
            pltpu.VMEM((nx, ny), F32),
            pltpu.VMEM((2, 2, nx, ny), F32),
            pltpu.VMEM((nx, ny), F32),
            pltpu.VMEM((nx, ny), F32),
            pltpu.SemaphoreType.DMA((6,)),
            pltpu.SemaphoreType.DMA((TICKS - 1, 2)),
            pltpu.SemaphoreType.DMA((TICKS - 1, 2)),
            pltpu.SemaphoreType.DMA((TICKS - 1,)),
            pltpu.SemaphoreType.DMA((TICKS - 1,)),
            pltpu.SemaphoreType.DMA((2,)),
            pltpu.SemaphoreType.DMA((2,)),
            pltpu.SemaphoreType.DMA,
            pltpu.SemaphoreType.DMA,
        ],
        compiler_params=pltpu.CompilerParams(collective_id=0, has_side_effects=True),
        name="slabs",
    )(fields, freq_index, slowness_index, slowness_table, jnp.asarray(xs), jnp.asarray(ys))
    return pl.pallas_call(
        store,
        out_shape=(
            jax.ShapeDtypeStruct((1, nx, ny), F32),
            jax.ShapeDtypeStruct(fields.shape, F32),
        ),
        in_specs=[vmem_spec, vmem_spec],
        out_specs=(any_spec, any_spec),
        scratch_shapes=[pltpu.SemaphoreType.DMA((2,))],
        name="store",
    )(
        pltpu.with_memory_space_constraint(image, pltpu.VMEM),
        pltpu.with_memory_space_constraint(moved, pltpu.VMEM),
    )


def solution(mesh):
    return jax.shard_map(
        body,
        mesh=mesh,
        in_specs=(
            P(("shots", "slab"), None, None, None, None),
            P(("shots", "slab")),
            P("slab", None, None),
            P(),
        ),
        out_specs=(P(("shots", "slab"), None, None), P(("shots", "slab"), None, None, None, None)),
        check_vma=False,
    )
```

```python
import functools
import math

import jax
import jax.numpy as jnp
import numpy as np
from jax import lax
from jax.experimental import pallas as pl
from jax.experimental.pallas import tpu as pltpu
from jax.sharding import PartitionSpec as P

TICKS = 3
NFREQ = 512

F32 = jnp.float32
BF16 = jnp.bfloat16
PI_HI = 3.140625
PI_LO = math.pi - 3.140625


def split_np(mat):
    high = mat.astype(BF16)
    low = (mat - high.astype(np.float64)).astype(BF16)
    return high, low


def dft_tables(nx, ny):
    half = ny // 2
    turn = np.outer(np.arange(nx), np.arange(nx)) % nx * (2.0 * np.pi / nx)
    c, s = np.cos(turn), np.sin(turn)
    x_mats = [np.block([[c, s], [-s, c]]), np.block([[c, -s], [s, c]]) / nx]
    y_mats = []
    for odd in (0, 1):
        turn = np.outer(np.arange(half), 2 * np.arange(half) + odd) % ny * (2.0 * np.pi / ny)
        c, s = np.cos(turn), np.sin(turn)
        y_mats.append(np.block([[c, -s], [s, c]]))
        y_mats.append(np.block([[c.T, s.T], [-s.T, c.T]]) / ny)
    xs = np.stack([part for mat in x_mats for part in split_np(mat)])
    ys = np.stack([part for mat in y_mats for part in split_np(mat)])
    return xs, ys


def split(value):
    high = value.astype(BF16)
    low = (value - high.astype(F32)).astype(BF16)
    return high, low


def dot_data_left(data, high, low):
    d_high, d_low = split(data)
    left = jnp.concatenate([d_high, d_low, d_high], axis=1)
    right = jnp.concatenate([high, high, low], axis=0)
    return jnp.dot(left, right, preferred_element_type=F32)


def dot_data_right(high, low, data):
    d_high, d_low = split(data)
    left = jnp.concatenate([high, high, low], axis=1)
    right = jnp.concatenate([d_high, d_low, d_high], axis=0)
    return jnp.dot(left, right, preferred_element_type=F32)


def sincos(x):
    turns = jnp.floor(x * (1.0 / math.pi) + 0.5)
    r = (x - turns * PI_HI) - turns * PI_LO
    sign = 1.0 - 2.0 * (turns - 2.0 * jnp.floor(turns * 0.5))
    r2 = r * r
    sin_p = 1.0 / math.factorial(11) * -1.0
    for k, sg in ((9, 1.0), (7, -1.0), (5, 1.0), (3, -1.0)):
        sin_p = sin_p * r2 + sg / math.factorial(k)
    sin_p = r + r * (r2 * sin_p)
    cos_p = 1.0 / math.factorial(12)
    for k, sg in ((10, -1.0), (8, 1.0), (6, -1.0), (4, 1.0), (2, -1.0), (0, 1.0)):
        cos_p = cos_p * r2 + sg / math.factorial(k)
    return sign * sin_p, sign * cos_p


def kernel(
    count, fields, freq_in, sidx, table, xs_in, ys_in, image_out, fields_out,
    held, made, plane, index, levels, xs, ys, raw, low, high, omegas,
    index_next, plane_next, ahead, bonus, part, freq,
    in_sems, send_sems, recv_sems, om_send, om_recv, im_send, im_recv, ix_send, ix_recv,
):
    me = lax.axis_index("slab")
    nx, ny = plane.shape
    half = ny // 2
    has_next = me < count - 1
    has_prev = me > 0
    nxt = jnp.minimum(me + 1, count - 1)
    prv = jnp.maximum(me - 1, 0)
    odd = lax.rem(me, 2) == 1
    looks_ahead = jnp.logical_and(odd, has_next)
    is_looked = jnp.logical_and(jnp.logical_not(odd), has_prev)

    loads = [
        pltpu.make_async_copy(table, levels, in_sems.at[0]),
        pltpu.make_async_copy(sidx.at[0], index, in_sems.at[1]),
        pltpu.make_async_copy(freq_in, freq, in_sems.at[2]),
        pltpu.make_async_copy(fields.at[0, 0], held.at[0, 0], in_sems.at[3]),
        pltpu.make_async_copy(xs_in, xs, in_sems.at[4]),
        pltpu.make_async_copy(ys_in, ys, in_sems.at[5]),
        pltpu.make_async_copy(fields.at[0, 1], held.at[0, 1], in_sems.at[6]),
    ]
    for load in loads:
        load.start()

    barrier = pltpu.get_barrier_semaphore()

    @pl.when(has_next)
    def _():
        pl.semaphore_signal(barrier, inc=1, device_id={"slab": nxt})

    @pl.when(has_prev)
    def _():
        pl.semaphore_signal(barrier, inc=1, device_id={"slab": prv})

    def field_copy(tick, f):
        return pltpu.make_async_remote_copy(
            src_ref=made.at[tick, f], dst_ref=held.at[tick + 1, f],
            send_sem=send_sems.at[tick, f], recv_sem=recv_sems.at[tick, f],
            device_id={"slab": nxt},
        )

    def omega_copy(tick):
        return pltpu.make_async_remote_copy(
            src_ref=omegas.at[tick], dst_ref=omegas.at[tick + 1],
            send_sem=om_send.at[tick], recv_sem=om_recv.at[tick],
            device_id={"slab": nxt},
        )

    def index_copy():
        return pltpu.make_async_remote_copy(
            src_ref=sidx.at[0], dst_ref=index_next,
            send_sem=ix_send, recv_sem=ix_recv, device_id={"slab": prv},
        )

    def image_copy(up, source=raw):
        return pltpu.make_async_remote_copy(
            src_ref=source, dst_ref=high if up else low,
            send_sem=im_send.at[up], recv_sem=im_recv.at[up],
            device_id={"slab": prv if up else nxt},
        )

    pl.semaphore_wait(barrier, (nxt - me) + (me - prv))

    @pl.when(is_looked)
    def _():
        index_copy().start()

    loads[2].wait()
    omegas[0] = jnp.full((8, 128), 1.0 + freq[0].astype(F32) / NFREQ, F32)

    @pl.when(has_next)
    def _():
        omega_copy(0).start()

    @pl.when(jnp.logical_not(has_prev))
    def _():
        held[1:] = jnp.zeros((TICKS - 1,) + held.shape[1:], F32)
        omegas[1:] = jnp.zeros((TICKS - 1, 8, 128), F32)
        low[...] = jnp.zeros((nx, ny), F32)

    @pl.when(jnp.logical_not(has_next))
    def _():
        high[...] = jnp.zeros((nx, ny), F32)

    for load in (loads[0], loads[1], loads[3], loads[4], loads[5]):
        load.wait()
    pieces = [
        jnp.broadcast_to(levels[pl.ds(j * 128, 128)].reshape(1, 128), (nx, 128))
        for j in range(levels.shape[0] // 128)
    ]

    def lookup(index, plane):
        for h in range(ny // 128):
            cols = pl.ds(h * 128, 128)
            idx = index[:, cols]
            inner = idx & 127
            value = jnp.take_along_axis(pieces[0], inner, axis=1, mode="promise_in_bounds")
            for j in range(1, len(pieces)):
                other = jnp.take_along_axis(pieces[j], inner, axis=1, mode="promise_in_bounds")
                value = jnp.where(idx >= j * 128, other, value)
            plane[:, cols] = value
        return jnp.sum(plane[...]) * (1.0 / (nx * ny))

    mean_slow = lookup(index, plane)

    row = lax.broadcasted_iota(jnp.int32, (nx, half), 0)
    wave_x = jnp.where(row < (nx + 1) // 2, row, row - nx).astype(F32) * (2.0 * math.pi / nx)
    lane = lax.broadcasted_iota(jnp.int32, (1, half), 1)

    def phases(omega, mean_slow):
        k_square = (omega * mean_slow) ** 2
        out = []
        for odd in (0, 1):
            k = 2 * lane + odd
            wave_y = jnp.where(k < (ny + 1) // 2, k, k - ny).astype(F32) * (2.0 * math.pi / ny)
            q = k_square - (wave_x * wave_x + wave_y * wave_y)
            root = jnp.sqrt(jnp.abs(q))
            sin_v, cos_v = sincos(root)
            moving = q > 0.0
            out.append((
                jnp.where(moving, cos_v, jnp.exp(-root)),
                jnp.where(moving, sin_v, 0.0),
            ))
        return out

    def step(source, target, f, phase, screen):
        re, im = source[f, 0], source[f, 1]
        sg = 1.0 if f == 0 else -1.0
        spec = dot_data_right(xs[0], xs[1], jnp.concatenate([re, im], axis=0))
        left, right = spec[:, :half], spec[:, half:]
        back = []
        for odd, mix in ((0, left + right), (1, left - right)):
            cos_p, sin_p = phase[odd]
            sin_p = sg * sin_p
            fwd = dot_data_left(
                jnp.concatenate([mix[:nx], mix[nx:]], axis=1), ys[4 * odd], ys[4 * odd + 1]
            )
            v_re, v_im = fwd[:, :half], fwd[:, half:]
            moved = jnp.concatenate(
                [v_re * cos_p - v_im * sin_p, v_re * sin_p + v_im * cos_p], axis=1
            )
            back.append(dot_data_left(moved, ys[4 * odd + 2], ys[4 * odd + 3]))
        plus, minus = back[0] + back[1], back[0] - back[1]
        cols = jnp.concatenate([
            jnp.concatenate([plus[:, :half], minus[:, :half]], axis=1),
            jnp.concatenate([plus[:, half:], minus[:, half:]], axis=1),
        ], axis=0)
        field = dot_data_right(xs[2], xs[3], cols)
        b_re, b_im = field[:nx], field[nx:]
        s_sin, s_cos = screen
        s_sin = sg * s_sin
        target[f, 0] = b_re * s_cos - b_im * s_sin
        target[f, 1] = b_re * s_sin + b_im * s_cos

    def moved_fields(tick):
        return made.at[tick] if tick < TICKS - 1 else fields_out.at[0]

    def factors(omega, plane, mean_slow):
        omega_wide = jnp.concatenate([omega] * (ny // 128), axis=1)
        return phases(omega, mean_slow), sincos(omega_wide * (plane[...] - mean_slow))

    for tick in range(TICKS):
        if tick > 0:
            @pl.when(has_prev)
            def _():
                omega_copy(tick - 1).wait_recv()

            if tick < TICKS - 1:
                @pl.when(has_next)
                def _():
                    omega_copy(tick).start()
        phase, screen = factors(omegas[tick][:1], plane, mean_slow)
        for f in (0, 1):
            if tick == 0 and f == 1:
                loads[6].wait()
            elif tick > 0:
                @pl.when(has_prev)
                def _():
                    field_copy(tick - 1, f).wait_recv()
            if tick == TICKS - 1 and f == 0:
                @pl.when(is_looked)
                def _():
                    image_copy(1, part).start()
            step(held.at[tick], moved_fields(tick), f, phase, screen)
            if tick < TICKS - 1:
                @pl.when(has_next)
                def _():
                    field_copy(tick, f).start()
        now = moved_fields(tick)
        added = now[0, 0] * now[1, 0] + now[0, 1] * now[1, 1]
        raw[...] = added if tick == 0 else raw[...] + added
        if tick == TICKS - 2:
            part[...] = raw[...]

            @pl.when(looks_ahead)
            def _():
                index_copy().wait_recv()
                mean_next = lookup(index_next, plane_next)
                phase, screen = factors(omegas[tick][:1], plane_next, mean_next)
                for f in (0, 1):
                    step(made.at[tick], ahead, f, phase, screen)
                bonus[...] = ahead[0, 0] * ahead[1, 0] + ahead[0, 1] * ahead[1, 1]

            @pl.when(jnp.logical_not(looks_ahead))
            def _():
                bonus[...] = jnp.zeros((nx, ny), F32)

    @pl.when(has_next)
    def _():
        image_copy(0).start()

    @pl.when(odd)
    def _():
        image_copy(1).start()

    @pl.when(has_prev)
    def _():
        image_copy(0).wait_recv()

    @pl.when(has_next)
    def _():
        image_copy(1).wait_recv()

    image_out[0] = raw[...] - 0.25 * (low[...] + (high[...] + bonus[...]))

    @pl.when(has_next)
    def _():
        for tick in range(TICKS - 1):
            omega_copy(tick).wait_send()
            for f in (0, 1):
                field_copy(tick, f).wait_send()
        image_copy(0).wait_send()

    @pl.when(odd)
    def _():
        image_copy(1).wait_send()

    @pl.when(is_looked)
    def _():
        index_copy().wait_send()
        image_copy(1, part).wait_send()


def store(image, fields, image_out, fields_out, sems):
    copies = [
        pltpu.make_async_copy(fields, fields_out, sems.at[0]),
        pltpu.make_async_copy(image, image_out, sems.at[1]),
    ]
    for copy in copies:
        copy.start()
    for copy in copies:
        copy.wait()


def body(fields, freq_index, slowness_index, slowness_table):
    nx, ny = slowness_index.shape[1:]
    assert slowness_index.shape[0] == 1
    xs, ys = dft_tables(nx, ny)
    count = lax.axis_size("slab")
    any_spec = pl.BlockSpec(memory_space=pl.ANY)
    vmem_spec = pl.BlockSpec(memory_space=pltpu.VMEM)
    image, moved = pl.pallas_call(
        functools.partial(kernel, count),
        out_shape=(pltpu.VMEM((1, nx, ny), F32), pltpu.VMEM(fields.shape, F32)),
        in_specs=[
            any_spec, any_spec, any_spec, any_spec, any_spec, any_spec,
        ],
        out_specs=(vmem_spec, vmem_spec),
        scratch_shapes=[
            pltpu.VMEM((TICKS, 2, 2, nx, ny), F32),
            pltpu.VMEM((TICKS - 1, 2, 2, nx, ny), F32),
            pltpu.VMEM((nx, ny), F32),
            pltpu.VMEM((nx, ny), jnp.int32),
            pltpu.VMEM(slowness_table.shape, F32),
            pltpu.VMEM(xs.shape, BF16),
            pltpu.VMEM(ys.shape, BF16),
            pltpu.VMEM((nx, ny), F32),
            pltpu.VMEM((nx, ny), F32),
            pltpu.VMEM((nx, ny), F32),
            pltpu.VMEM((TICKS, 8, 128), F32),
            pltpu.VMEM((nx, ny), jnp.int32),
            pltpu.VMEM((nx, ny), F32),
            pltpu.VMEM((2, 2, nx, ny), F32),
            pltpu.VMEM((nx, ny), F32),
            pltpu.VMEM((nx, ny), F32),
            pltpu.SMEM(freq_index.shape, jnp.int32),
            pltpu.SemaphoreType.DMA((7,)),
            pltpu.SemaphoreType.DMA((TICKS - 1, 2)),
            pltpu.SemaphoreType.DMA((TICKS - 1, 2)),
            pltpu.SemaphoreType.DMA((TICKS - 1,)),
            pltpu.SemaphoreType.DMA((TICKS - 1,)),
            pltpu.SemaphoreType.DMA((2,)),
            pltpu.SemaphoreType.DMA((2,)),
            pltpu.SemaphoreType.DMA,
            pltpu.SemaphoreType.DMA,
        ],
        compiler_params=pltpu.CompilerParams(collective_id=0, has_side_effects=True),
        name="slabs",
    )(fields, freq_index, slowness_index, slowness_table, jnp.asarray(xs), jnp.asarray(ys))
    return pl.pallas_call(
        store,
        out_shape=(
            jax.ShapeDtypeStruct((1, nx, ny), F32),
            jax.ShapeDtypeStruct(fields.shape, F32),
        ),
        in_specs=[vmem_spec, vmem_spec],
        out_specs=(any_spec, any_spec),
        scratch_shapes=[pltpu.SemaphoreType.DMA((2,))],
        name="store",
    )(
        pltpu.with_memory_space_constraint(image, pltpu.VMEM),
        pltpu.with_memory_space_constraint(moved, pltpu.VMEM),
    )


def solution(mesh):
    return jax.shard_map(
        body,
        mesh=mesh,
        in_specs=(
            P(("shots", "slab"), None, None, None, None),
            P(("shots", "slab")),
            P("slab", None, None),
            P(),
        ),
        out_specs=(P(("shots", "slab"), None, None), P(("shots", "slab"), None, None, None, None)),
        check_vma=False,
    )
```
